32 devices in a mesh: study: 2 (over x), vol: 8 (over z, y), tile: 2 (over core).
Axes of the slice: x: 2, y: 2, z: 4, core: 2. Of those that a mesh axis runs over, the one named last changes fastest.
Arguments:
- spectra: bfloat16 [16, 4, 768, 2048], P(('study', 'vol'), None, 'tile'), parts along dimension 0, may hold values from -6 to 6
- block_scales: float32 [16, 4, 768, 16], P(('study', 'vol'), None, 'tile'), parts along dimension 0, may hold values from 0.3 to 3
- retina_blocks: int32 [12, 2], P(('study', 'tile')), parts along dimension 0, may hold values from 0 to 3, as said below
- quality_block: int32 [16, 6], P(('study', 'vol'), 'tile'), parts along dimension 0, may hold values from 0 to 3, as said below
- quality_bias: float32 [16, 6], P(('study', 'vol'), 'tile'), parts along dimension 0, may hold values from -110 to 160
Outputs:
- angiogram: float32 [1024, 768], P(('study', 'vol'), 'tile'), parts along dimension 0
- joined_structure: float32 [1024, 768], P(('study', 'vol'), 'tile'), parts along dimension 0
- spread_map: float32 [1024, 768], P(('study', 'vol'), 'tile'), parts along dimension 0
The draws below stay inside these ranges and needn't reach their ends.
There are 2 independent parts, one for each index of `study`. The reference program is written for one: setup_inputs(seed, part) draws one part's arguments, and reference() takes and returns one part's arrays. A program takes and returns all parts, laid end to end along the dimension named above; each array names one. Nothing has to cross between parts.
Inputs may be any that keep to these rules, and one draw needn't show every extreme that they name: retina_blocks[j,0] <= retina_blocks[j,1]. quality_block[v,j] lies between retina_blocks[j,0] and retina_blocks[j,1].
All inputs are finite; a program needn't handle non-finite values.
Results may differ from the reference program's by a relative error of at most 0.0015.
Values sent between devices are 32-bit elements; how exact they have to be, the bound alone decides.
A program may use at most 128 MiB of HBM per device.

```python
import math
import jax
import jax.numpy as jnp
from jax import lax

K = 2048
DEPTH = 512
BANDS = 4
REPEATS = 4
DBLK = 128
ABLK = 128
SB = 128
ALINES = 768
VOLS = 8
ABLKS = 6
KB = 16
NDB = 4


def draw_pattern(key):
    key_first = jax.random.fold_in(key, 101)
    key_last = jax.random.fold_in(key, 102)
    key_zero = jax.random.fold_in(key, 103)
    key_top = jax.random.fold_in(key, 104)
    first_block = jax.random.randint(key_first, (ABLKS,), 0, NDB // 2)
    last_block = jax.random.randint(key_last, (ABLKS,), NDB // 2, NDB)
    zero_at = jax.random.randint(key_zero, (), 0, ABLKS)
    top_at = jax.random.randint(key_top, (), 0, ABLKS)
    tile_index = jnp.arange(ABLKS, dtype=jnp.int32)
    first_block = jnp.where(tile_index == zero_at, 0, first_block)
    last_block = jnp.where(tile_index == top_at, NDB - 1, last_block)
    return (first_block.astype(jnp.int32), last_block.astype(jnp.int32), zero_at, top_at)


def draw_retina_blocks(key, part):
    first_block, last_block, zero_at, top_at = draw_pattern(key)
    return jnp.stack([first_block, last_block], axis=1).astype(jnp.int32)


def draw_quality_block(key, part):
    first_block, last_block, zero_at, top_at = draw_pattern(key)
    key_pick = jax.random.fold_in(key, 7)
    key_volume = jax.random.fold_in(key, 8)
    raw_pick = jax.random.randint(key_pick, (VOLS, ABLKS), 0, NDB)
    chosen = first_block[None, :] + raw_pick % (last_block - first_block + 1)[None, :]
    low_volume = jax.random.randint(key_volume, (), 0, VOLS)
    high_volume = (low_volume + 1) % VOLS
    volume_index = jnp.arange(VOLS, dtype=jnp.int32)[:, None]
    tile_index = jnp.arange(ABLKS, dtype=jnp.int32)[None, :]
    chosen = jnp.where((volume_index == low_volume) & (tile_index == zero_at), 0, chosen)
    chosen = jnp.where((volume_index == high_volume) & (tile_index == top_at), NDB - 1, chosen)
    return chosen.astype(jnp.int32)


def draw_quality_bias(key, part):
    return jax.random.uniform(key, (VOLS, ABLKS), jnp.float32, -2.0, 2.0)


def block_scale(rng, dims, shards, least, largest):
    level, own = 1.0, jax.random.fold_in(rng, 6)
    for position, parts in shards:
        draws = jnp.exp(jax.random.uniform(jax.random.fold_in(own, position), (parts,), jnp.float32, least / len(shards), largest / len(shards)))
        level = level * jnp.repeat(draws, dims[position] // parts).reshape([-1 if axis == position else 1 for axis in range(len(dims))])
    return level


def normal_values(own_key, shape, spread, reach, split=(), kind=jnp.bfloat16):
    values = jax.random.normal(own_key, shape, jnp.float32) * spread
    if len(split) > 0:
        values = block_scale(own_key, shape, split, -0.22, 0.18) * values
    return jnp.clip(values, min=-reach, max=reach).astype(kind)


def setup_inputs(seed: int = 0, part: int = 0) -> dict:
    streams_of = jax.random.split(jax.random.key(seed), 6)
    own_keys = jax.random.split(jax.random.fold_in(streams_of[5], part), 6)
    spectra = normal_values(own_keys[0], (VOLS, REPEATS, ALINES, K), 1.0, 6.0, ((0, 8), (2, 2)))
    block_scales = jnp.clip(jnp.exp(math.log(3.0) - 2.3025851 * jax.random.uniform(own_keys[1], (VOLS, REPEATS, ALINES, KB), jnp.float32) ** block_scale(own_keys[1], (VOLS, REPEATS, ALINES, KB), ((0, 8), (2, 2)), -0.2, 0.2)), 0.3, 3.0)
    retina_blocks = draw_retina_blocks(jax.random.fold_in(jax.random.fold_in(streams_of[5], part), 71), part)
    quality_block = draw_quality_block(jax.random.fold_in(jax.random.fold_in(streams_of[5], part), 71), part)
    quality_bias = draw_quality_bias(jax.random.fold_in(jax.random.fold_in(streams_of[5], part), 71), part)
    return {"spectra": spectra, "block_scales": block_scales, "retina_blocks": retina_blocks, "quality_block": quality_block, "quality_bias": quality_bias}


smooth_taps = (1.0 / 9.0, 2.0 / 9.0, 3.0 / 9.0, 2.0 / 9.0, 1.0 / 9.0)

def window_tables():
    sample_index = jnp.arange(K, dtype=jnp.int32)
    depth_index = jnp.arange(DEPTH, dtype=jnp.int32)
    phase_angle = (sample_index[:, None] * depth_index[None, :] % K).astype(jnp.float32) * (2.0 * math.pi / K)
    kernel = jnp.stack([jnp.cos(phase_angle), -jnp.sin(phase_angle)], axis=1)
    centres = (jnp.arange(BANDS, dtype=jnp.float32)[:, None] + 0.5) * (K / BANDS)
    distance = sample_index.astype(jnp.float32)[None, :] - centres
    offsets = distance / (K / 8.0)
    window = jnp.where(jnp.abs(distance) <= K / 2.0, jnp.exp(-0.5 * offsets * offsets), 0.0)
    window = window / jnp.sqrt(lax.optimization_barrier(jnp.sum(window * window, axis=1, keepdims=True)))
    return (window[:, :, None, None] * kernel[None]).astype(jnp.bfloat16)

def spread_columns(values, repeat_width):
    widened = jnp.broadcast_to(values[..., None], values.shape + (repeat_width,))
    return widened.reshape(values.shape[:-1] + (values.shape[-1] * repeat_width,))

def scale_spectra(spectra_vol, scales_vol):
    shaped = spectra_vol.astype(jnp.float32).reshape(scales_vol.shape + (SB,))
    return (shaped * scales_vol[..., None]).reshape(spectra_vol.shape).astype(jnp.bfloat16)

def band_maps(scaled, tables):
    line_count = scaled.shape[1]
    decorrelation = jnp.zeros((DEPTH, line_count), jnp.float32)
    power_total = jnp.zeros((DEPTH, line_count), jnp.float32)
    for band_index in range(BANDS):
        fields = jnp.einsum('kcd,rak->cdra', tables[band_index].astype(jnp.float32), scaled.astype(jnp.float32))
        band_power = fields[0] * fields[0] + fields[1] * fields[1]
        amplitude = jnp.sqrt(band_power + 0.05)
        pair_ratio = 2.0 * amplitude[:, :-1] * amplitude[:, 1:] / (band_power[:, :-1] + band_power[:, 1:] + 0.1)
        decorrelation = decorrelation + lax.optimization_barrier(jnp.sum(1.0 - pair_ratio, axis=1))
        power_total = power_total + lax.optimization_barrier(jnp.sum(band_power, axis=1))
    decorrelation = decorrelation / (BANDS * (REPEATS - 1))
    structure = jnp.log(power_total / (BANDS * REPEATS) + 0.1)
    return (decorrelation, structure)

def retina_mask(first_col, last_col):
    depth_block = jnp.arange(DEPTH, dtype=jnp.int32) // DBLK
    return (depth_block[:, None] >= first_col[None, :]) & (depth_block[:, None] <= last_col[None, :])

def lateral_smooth(padded, line_count):
    filtered = smooth_taps[0] * padded[:, 0:line_count]
    for offset_index in range(1, 5):
        filtered = filtered + smooth_taps[offset_index] * padded[:, offset_index:offset_index + line_count]
    return filtered

def block_quality(structure, qblock):
    tile_count = qblock.shape[0]
    block_means = lax.optimization_barrier(jnp.mean(structure.reshape(NDB, DBLK, tile_count, ABLK), axis=(1, 3)))
    chosen = jnp.arange(NDB, dtype=jnp.int32)[:, None] == qblock[None, :]
    return lax.optimization_barrier(jnp.sum(jnp.where(chosen, block_means, 0.0), axis=0))

def reference(spectra, block_scales, retina_blocks, quality_block, quality_bias):
    tables = window_tables()
    first_col = spread_columns(retina_blocks[:, 0], ABLK)
    last_col = spread_columns(retina_blocks[:, 1], ABLK)
    inside = retina_mask(first_col, last_col)

    def per_volume(volume_items):
        spectra_vol, scales_vol, qblock, bias_row = volume_items
        scaled = scale_spectra(spectra_vol, scales_vol)
        decorrelation, structure = band_maps(scaled, tables)
        masked_decorrelation = jnp.where(inside, decorrelation, 0.0)
        masked_structure = jnp.where(inside, structure, 0.0)
        padded = jnp.pad(masked_decorrelation, ((0, 0), (2, 2)))
        smoothed = lateral_smooth(padded, ALINES)
        volume_score = block_quality(structure, qblock) + bias_row
        return (smoothed, masked_structure, volume_score)
    smoothed, structures, scores = lax.map(per_volume, (spectra, block_scales, quality_block, quality_bias))
    weights = jnp.exp(scores - lax.optimization_barrier(jnp.max(scores, axis=0, keepdims=True)))
    weights = weights / lax.optimization_barrier(jnp.sum(weights, axis=0, keepdims=True))
    column_weights = spread_columns(weights, ABLK)[:, None, :]
    angiogram = lax.optimization_barrier(jnp.sum(column_weights * smoothed, axis=0))
    second_moment = lax.optimization_barrier(jnp.sum(column_weights * smoothed * smoothed, axis=0))
    joined_structure = lax.optimization_barrier(jnp.sum(column_weights * structures, axis=0))
    spread_map = jnp.sqrt(second_moment - angiogram * angiogram + 0.01)
    return (angiogram, joined_structure, spread_map)
```

```python
import functools
import math

import jax
import jax.numpy as jnp
from jax import lax
from jax.experimental import pallas as pl
from jax.experimental.pallas import tpu as pltpu
from jax.sharding import PartitionSpec as P

DEPTH = 512
BANDS = 4
DBLK = 128
ABLK = 128
SB = 128
NDB = 4
CLASSES = 8
MESH = pl.DeviceIdType.MESH
PART = 32
PARTS = DBLK // PART
GROUPS = PART // 8
UNROLL = 4
SPREAD = 2
HEAD = BANDS * 2 * PART
LHS = HEAD + 16


def turn(re, im, cre, cim):
    return re * cre - im * cim, re * cim + im * cre


def build_trig(wins, trig, steps, perm, samples):
    inner = samples // CLASSES
    unit = 2.0 * math.pi / samples
    kk = (
        lax.broadcasted_iota(jnp.int32, (CLASSES, inner), 1) * CLASSES
        + lax.broadcasted_iota(jnp.int32, (CLASSES, inner), 0)
    ).astype(jnp.float32)
    for k0 in range(CLASSES):
        wins[k0] = jnp.zeros((8, inner), jnp.float32)
    for b in range(BANDS):
        distance = kk - (b + 0.5) * (samples / BANDS)
        offset = distance / (samples / 8.0)
        g = jnp.where(jnp.abs(distance) <= samples / 2.0, jnp.exp(-0.5 * offset * offset), 0.0)
        g = g / jnp.sqrt(jnp.sum(g * g, keepdims=True))
        for k0 in range(CLASSES):
            wins[k0, b : b + 1, :] = g[k0 : k0 + 1]
    z = lax.broadcasted_iota(jnp.int32, (8, inner), 0)
    k1 = lax.broadcasted_iota(jnp.int32, (8, inner), 1)
    angle = ((CLASSES * k1 * z) % samples).astype(jnp.float32) * unit
    trig[0, :8], trig[1, :8] = jnp.cos(angle), -jnp.sin(angle)
    angle = ((CLASSES * k1 * 8) % samples).astype(jnp.float32) * unit
    cre, cim = jnp.cos(angle), -jnp.sin(angle)
    angle = z.astype(jnp.float32)[:, :128] * unit
    steps[0, :8], steps[1, :8] = jnp.cos(angle), -jnp.sin(angle)
    have = 8
    while have < DBLK:
        for at in range(0, have, 8):
            to = pl.ds(have + at, 8)
            trig[0, to], trig[1, to] = turn(trig[0, at : at + 8], trig[1, at : at + 8], cre, cim)
            steps[0, to], steps[1, to] = turn(
                steps[0, at : at + 8],
                steps[1, at : at + 8],
                math.cos(have * unit),
                -math.sin(have * unit),
            )
        cre, cim = turn(cre, cim, cre, cim)
        have *= 2
    last = pl.ds(DBLK, 8)
    trig[0, last], trig[1, last] = cre, cim
    steps[0, last] = jnp.full((8, 128), math.cos(DBLK * unit), jnp.float32)
    steps[1, last] = jnp.full((8, 128), -math.sin(DBLK * unit), jnp.float32)
    size = perm.shape[0]
    part = size // CLASSES
    row = lax.broadcasted_iota(jnp.int32, (size, size), 0)
    col = lax.broadcasted_iota(jnp.int32, (size, size), 1)
    perm[...] = jnp.where(col == (row % part) * CLASSES + row // part, 1.0, 0.0).astype(jnp.bfloat16)


def build_class(table, wins, trig, steps, k0):
    inner = trig.shape[2]
    rows = [wins[k0, b : b + 1, :] for b in range(BANDS)]
    for p in range(PARTS):
        at = pl.ds(p * PART, PART)
        for c in range(2):
            value = trig[c, at]
            for b in range(BANDS):
                to = pl.ds((b * 2 + c) * PART, PART)
                table[p, k0, to, :] = (value * rows[b]).astype(jnp.bfloat16)
    last = pl.ds(DBLK, 8)
    both = jnp.concatenate([trig[c, last] * wins[k0] for c in range(2)], axis=0)
    for p in range(PARTS):
        table[p, k0, HEAD:LHS, :] = both.astype(jnp.bfloat16)
    for at in range(0, DBLK + 8, 8):
        here = pl.ds(at, 8)
        sre = jnp.concatenate([steps[0, here]] * (inner // 128), axis=1)
        sim = jnp.concatenate([steps[1, here]] * (inner // 128), axis=1)
        trig[0, here], trig[1, here] = turn(trig[0, here], trig[1, here], sre, sim)


def combine(get):
    rr, ii = [get(k, 0) for k in range(8)], [get(k, 1) for k in range(8)]
    sr = [rr[j] + rr[j + 4] for j in range(4)]
    si = [ii[j] + ii[j + 4] for j in range(4)]
    dr = [rr[j] - rr[j + 4] for j in range(4)]
    di = [ii[j] - ii[j + 4] for j in range(4)]
    half = math.sqrt(0.5)
    re0, im0 = (sr[0] + sr[2]) + (sr[1] + sr[3]), (si[0] + si[2]) + (si[1] + si[3])
    re3, im3 = (sr[0] - sr[2]) - (si[1] - si[3]), (si[0] - si[2]) + (sr[1] - sr[3])
    p, q = (dr[1] - dr[3]) * half, (di[1] + di[3]) * half
    r, t = (di[1] - di[3]) * half, (dr[1] + dr[3]) * half
    re2, im2 = (dr[0] + di[2]) + (p + q), (di[0] - dr[2]) + (r - t)
    re1, im1 = (dr[0] - di[2]) + (p - q), (di[0] + dr[2]) + (r + t)
    fields = ((re0, im0), (re1, im1), (re2, im2), (re3, im3))
    return [re * re + (im * im + 0.05) for re, im in fields]


def ratio_and_total(powers, d):
    total = powers[0][d]
    ratio = None
    for first, second in zip(powers[:-1], powers[1:]):
        first, second = first[d], second[d]
        total = total + second
        prod, both = first * second, first + second
        term = prod * lax.rsqrt(prod * (both * both))
        ratio = term if ratio is None else ratio + term
    return ratio, total


def tile_at(step, tiles):
    t = lax.axis_index("tile")
    return (tiles - 1 - step) + t * (2 * step - tiles + 1)


def fused_kernel(
    retina, qblock, bias, spec, scales, joined_out,
    xin, factors, table, wins, trig, steps, perm, da, db, ga, gb, prev, score_acc,
    sent, got, score_sent, score_got, part_sent, part_got, part_near, redge,
    fix_sent, fix_got, fix_near,
    isem, ssem, rsem, csem, dsem, psem, qsem, lsem, esem, fsem,
):
    tiles, repeats, lines, samples = xin.shape
    chunk = perm.shape[0]
    chunks = samples // chunk
    n = score_got.shape[1]
    half = n // 2
    rows = redge.shape[2]
    me, t = lax.axis_index("vol"), lax.axis_index("tile")
    other = 1 - t
    side, place = me // half, me % half
    part = chunk // CLASSES
    cols = repeats * lines

    data, g = (da, db), (ga, gb)

    def load(step):
        at = pl.ds(pl.multiple_of(tile_at(step, tiles) * lines, lines), lines)
        return pltpu.make_async_copy(spec.at[0, :, at, :], xin.at[step], isem.at[step])

    for step in range(tiles):
        load(step).start()
    barrier = pltpu.get_barrier_semaphore()
    for d in range(1, n):
        pl.semaphore_signal(barrier, inc=1, device_id={"vol": (me + d) % n}, device_id_type=MESH)
    pl.semaphore_signal(barrier, inc=1, device_id={"tile": other}, device_id_type=MESH)
    build_trig(wins, trig, steps, perm, samples)
    per = chunk // SB
    for step in range(tiles):
        lane = pl.ds(pl.multiple_of(tile_at(step, tiles) * lines, lines), lines)
        for r in range(repeats):
            block = scales[0, r, :, lane]
            for q in range(chunks):
                factors[step, q, :per, r * lines : (r + 1) * lines] = block[q * per : (q + 1) * per]

    def prepare(step, q):
        at = pl.ds(q * chunk if isinstance(q, int) else pl.multiple_of(q * chunk, chunk), chunk)
        block = xin[step, :, :, at].reshape(cols, chunk)
        moved = lax.dot_general(
            perm[...], block, (((1,), (1,)), ((), ())), preferred_element_type=jnp.float32
        )
        factor = jnp.concatenate(
            [
                jnp.broadcast_to(factors[step, q, h : h + 1, :], (part // per, cols))
                for h in range(per)
            ],
            axis=0,
        )
        to = pl.ds(q * part if isinstance(q, int) else pl.multiple_of(q * part, part), part)
        for k0 in range(CLASSES):
            data[step % 2][k0, to, :] = (moved[k0 * part : (k0 + 1) * part] * factor).astype(
                jnp.bfloat16
            )

    def multiply(step, p, slot, k0):
        g[slot][k0] = jnp.dot(
            table[p, k0], data[step % 2][k0], preferred_element_type=jnp.float32
        )

    sub = lax.broadcasted_iota(jnp.int32, (8, lines), 0)
    backwards = (8 - sub) % 8

    def dec_of(ratio):
        return 1.0 - ratio * (2.0 / (BANDS * (repeats - 1)))

    def struct_of(total):
        return jnp.log(total * (1.0 / (BANDS * repeats)) + 0.05)

    def lanes(r):
        return slice(r * lines, (r + 1) * lines)

    def reduce_last(slot):
        powers = [
            combine(lambda k, c: g[slot][k, HEAD + c * 8 : HEAD + c * 8 + 8, lanes(r)])
            for r in range(repeats)
        ]
        for d in (1, 3):
            ratio, total = ratio_and_total(powers, d)
            ratio = jnp.sum(ratio[:BANDS], axis=0, keepdims=True)
            total = jnp.sum(total[:BANDS], axis=0, keepdims=True)
            prev[d // 2, 0] = jnp.broadcast_to(dec_of(ratio), (8, lines))
            prev[d // 2, 1] = jnp.broadcast_to(struct_of(total), (8, lines))

    def reduce(step, p, slot, i):
        here = tile_at(step, tiles)
        first, last, rated = retina[0, here], retina[1, here], qblock[0, here]
        at = (GROUPS - 1 - i) * 8 if UNROLL == GROUPS else pl.multiple_of((GROUPS - 1 - i) * 8, 8)
        ratios, totals = [None] * NDB, [None] * NDB
        for b in range(BANDS):
            powers = [
                combine(lambda k, c: g[slot][k, pl.ds((b * 2 + c) * PART + at, 8), lanes(r)])
                for r in range(repeats)
            ]
            for d in range(NDB):
                ratio, total = ratio_and_total(powers, d)
                ratios[d] = ratio if b == 0 else ratios[d] + ratio
                totals[d] = total if b == 0 else totals[d] + total
        score = score_acc[...]
        for d in range(NDB):
            dec, struct = dec_of(ratios[d]), struct_of(totals[d])
            to = at
            if d % 2:
                low_dec, low_struct = prev[d // 2, 0], prev[d // 2, 1]
                prev[d // 2, 0] = dec
                prev[d // 2, 1] = struct
                dec = jnp.where(sub == 0, low_dec, jnp.take_along_axis(dec, backwards, axis=0))
                struct = jnp.where(
                    sub == 0, low_struct, jnp.take_along_axis(struct, backwards, axis=0)
                )
                to = i * 8 if UNROLL == GROUPS else pl.multiple_of(i * 8, 8)
            inside = (first <= d) & (d <= last)
            score = score + jnp.where(rated == d, struct, 0.0)
            sent[step, p, d, 0, pl.ds(to, 8), :] = jnp.where(inside, dec, 0.0)
            sent[step, p, d, 1, pl.ds(to, 8), :] = jnp.where(inside, struct, 0.0)
        score_acc[...] = score

    def goes_to(p, d):
        depth = d * DBLK + (DBLK - PART - p * PART if d % 2 else p * PART)
        u = depth // rows
        return u // half, u % half, depth % rows

    def maps(step, p, d):
        far, target, at = goes_to(p, d)
        return pltpu.make_async_remote_copy(
            src_ref=sent.at[step, p, d],
            dst_ref=got.at[step, place, far, :, pl.ds(at, PART), :],
            send_sem=ssem.at[step], recv_sem=rsem.at[step, place],
            device_id={"vol": side * half + target}, device_id_type=MESH,
        )

    def own_maps(step, p, d):
        far, target, at = goes_to(p, d)
        return pltpu.make_async_copy(
            sent.at[step, p, d], got.at[step, place, far, :, pl.ds(at, PART), :],
            lsem.at[0, step],
        )

    def arrived(step, source):
        return pltpu.make_async_remote_copy(
            src_ref=got.at[step, source], dst_ref=got.at[step, source],
            send_sem=ssem.at[step], recv_sem=rsem.at[step, source],
            device_id={"vol": side * half + source}, device_id_type=MESH,
        )

    def all_sent(step):
        those = got.at[step, pl.ds(0, half - 1)]
        return pltpu.make_async_remote_copy(
            src_ref=those, dst_ref=those,
            send_sem=ssem.at[step], recv_sem=rsem.at[step, 0],
            device_id={"vol": (me + 1) % n}, device_id_type=MESH,
        )

    def own_arrived(step):
        return pltpu.make_async_copy(got.at[step, place], got.at[step, place], lsem.at[0, step])

    def score_to(step, d):
        return pltpu.make_async_remote_copy(
            src_ref=score_sent.at[step], dst_ref=score_got.at[step, me],
            send_sem=csem.at[step], recv_sem=dsem.at[step, me],
            device_id={"vol": (me + d) % n}, device_id_type=MESH,
        )

    def group_score_from(step, d):
        source = side * half + (place + d) % half
        return pltpu.make_async_remote_copy(
            src_ref=score_sent.at[step], dst_ref=score_got.at[step, source],
            send_sem=csem.at[step], recv_sem=dsem.at[step, source],
            device_id={"vol": source}, device_id_type=MESH,
        )

    def other_score_from(step, d):
        source = (1 - side) * half + (place + d) % half
        return pltpu.make_async_remote_copy(
            src_ref=score_sent.at[step], dst_ref=score_got.at[step, source],
            send_sem=csem.at[step], recv_sem=dsem.at[step, source],
            device_id={"vol": source}, device_id_type=MESH,
        )

    def scores_sent(step):
        those = score_got.at[step, pl.ds(0, n - 1)]
        return pltpu.make_async_remote_copy(
            src_ref=those, dst_ref=those,
            send_sem=csem.at[step], recv_sem=dsem.at[step, 0],
            device_id={"vol": (me + 1) % n}, device_id_type=MESH,
        )

    def partial(step):
        return pltpu.make_async_remote_copy(
            src_ref=part_sent.at[step], dst_ref=part_got.at[step],
            send_sem=psem.at[step], recv_sem=qsem.at[step],
            device_id={"vol": (1 - side) * half + place}, device_id_type=MESH,
        )

    fixes = pltpu.make_async_remote_copy(
        src_ref=fix_sent, dst_ref=fix_got, send_sem=fsem.at[0], recv_sem=fsem.at[1],
        device_id={"vol": (1 - side) * half + place}, device_id_type=MESH,
    )

    edge = pltpu.make_async_remote_copy(
        src_ref=got.at[0, :, :, 0], dst_ref=redge,
        send_sem=esem.at[0], recv_sem=esem.at[1],
        device_id={"tile": other}, device_id_type=MESH,
    )

    def send_part(step, p):
        for d in range(NDB):
            _, target, _ = goes_to(p, d)

            @pl.when(place != target)
            def _():
                maps(step, p, d).start()

            @pl.when(place == target)
            def _():
                own_maps(step, p, d).start()

    lane = lax.broadcasted_iota(jnp.int32, (8, lines), 1)
    facing = jnp.where(t == 0, lane, lines - 1 - lane) < 2

    def send_score(step):
        total = jnp.sum(score_acc[...], axis=0, keepdims=True)
        mean = jnp.sum(total, axis=1, keepdims=True) * (1.0 / (DBLK * lines))
        mean = mean + bias[0, tile_at(step, tiles)]
        score_sent[step] = jnp.broadcast_to(mean, (8, lines))
        for d in range(1, n):
            score_to(step, d).start()
        pltpu.make_async_copy(
            score_sent.at[step], score_got.at[step, me], lsem.at[1, step]
        ).start()

    def arrive(step):
        own_arrived(step).wait()
        pltpu.make_async_copy(
            score_sent.at[step], score_got.at[step, me], lsem.at[1, step]
        ).wait()
        for d in range(1, half):
            group_score_from(step, d).wait_recv()
        for d in range(1, half):
            arrived(step, (place + d) % half).wait_recv()

    def group_weights(step, at):
        ratings = [score_got[step, at * half + v, :1, :] for v in range(half)]
        top = functools.reduce(jnp.maximum, ratings)
        return top, [jnp.exp(x - top) for x in ratings]

    def shares(step):
        near_top, near_weights = group_weights(step, side)
        far_top, far_weights = group_weights(step, 1 - side)
        top = jnp.maximum(near_top, far_top)
        near, far = jnp.exp(near_top - top), jnp.exp(far_top - top)
        total = near * functools.reduce(jnp.add, near_weights)
        total = total + far * functools.reduce(jnp.add, far_weights)
        return near / total, far / total

    def smooth_of(step, v, to, at, with_next):
        own = got[step, v, to, 0, pl.ds(at, 8), :]
        if step:
            inner = got[step - 1, v, to, 0, pl.ds(at, 8), :]
        else:
            inner = redge[v, to, pl.ds(at, 8), :]
        outer = got[step + 1, v, to, 0, pl.ds(at, 8), :] if with_next else 0.0
        near_right = jnp.where(lane < lines // 2, jnp.where(t == 0, inner, outer), own)
        near_left = jnp.where(lane < lines // 2, own, jnp.where(t == 0, outer, inner))
        right2 = pltpu.roll(jnp.where(lane >= lines - 2, near_left, own), 2, 1)
        right1 = pltpu.roll(jnp.where(lane >= lines - 1, near_left, own), 1, 1)
        left1 = pltpu.roll(jnp.where(lane < 1, near_right, own), lines - 1, 1)
        left2 = pltpu.roll(jnp.where(lane < 2, near_right, own), lines - 2, 1)
        return (
            (right2 + left2) * (1.0 / 9.0) + (right1 + left1) * (2.0 / 9.0) + own * (3.0 / 9.0)
        )

    def add_up(step):
        _, weights = group_weights(step, side)
        for far in range(2):
            to = 1 - side if far else side
            store = part_sent if far else part_near
            for at in range(0, rows, 8):
                ang = square = joined = 0.0
                for v in range(half):
                    smooth = smooth_of(step, v, to, at, False)
                    ws = weights[v] * smooth
                    ang = ang + ws
                    square = square + ws * smooth
                    joined = joined + weights[v] * got[step, v, to, 1, pl.ds(at, 8), :]
                store[step, 0, at : at + 8, :] = ang
                store[step, 1, at : at + 8, :] = square
                store[step, 2, at : at + 8, :] = joined
        partial(step).start()

    def fix_at(step, k, i):
        return (step * 2 + k) * (rows // 8) + i

    assert 2 * fix_at(max(tiles - 2, 0), 1, rows // 8 - 1) + 2 <= lines

    def fix_up(step):
        _, weights = group_weights(step, side)
        for far in range(2):
            to = 1 - side if far else side
            store = fix_sent if far else fix_near
            packed = store[...] if step else jnp.zeros((8, lines), jnp.float32)
            for i in range(rows // 8):
                ang = square = 0.0
                for v in range(half):
                    smooth = smooth_of(step, v, to, i * 8, True)
                    ws = weights[v] * smooth
                    ang = ang + ws
                    square = square + ws * smooth
                for k, value in enumerate((ang, square)):
                    value = jnp.where(t == 0, value, pltpu.roll(value, 2, 1))
                    place_at = fix_at(step, k, i)
                    moved = pltpu.roll(value, 2 * place_at, 1) if place_at else value
                    packed = jnp.where(lane // 2 == place_at, moved, packed)
            store[...] = packed

    load(0).wait()

    def first_pass(k0, carry):
        build_class(table, wins, trig, steps, k0)
        prepare(0, k0)
        return carry

    assert chunks == CLASSES and GROUPS == SPREAD * (chunks // PARTS)
    for k0 in range(CLASSES):
        first_pass(k0, 0)
    for k0 in range(CLASSES):
        multiply(0, PARTS - 1, 0, k0)
    for step in range(1, tiles):
        load(step).wait()
    if tiles > 1:
        for q in range(chunks // PARTS):
            prepare(1, q)

    slot = 0
    each = CLASSES // GROUPS
    for step in range(tiles):
        score_acc[...] = jnp.zeros_like(score_acc)
        reduce_last(slot)
        for turn_at in range(PARTS):
            p = PARTS - 1 - turn_at
            if turn_at + 1 < PARTS:
                following = (step, p - 1)
            elif step + 1 < tiles:
                following = (step + 1, PARTS - 1)
            else:
                following = None

            if turn_at + 1 < PARTS:
                ready, first_chunk = step + 1, (turn_at + 1) * (chunks // PARTS)
            else:
                ready, first_chunk = step + 2, 0
            if ready >= tiles:
                ready = None

            def body(trip, carry):
                for inner_trip in range(UNROLL):
                    i = trip * UNROLL + inner_trip
                    if following is not None:
                        for k in range(each):
                            multiply(*following, 1 - slot, i * each + k)
                    if ready is not None and (inner_trip + 1) % SPREAD == 0:
                        prepare(ready, first_chunk + (trip * UNROLL + inner_trip) // SPREAD)
                    reduce(step, p, slot, i)
                return carry

            if UNROLL == GROUPS:
                body(0, 0)
            else:
                lax.fori_loop(0, GROUPS // UNROLL, body, 0)
            slot = 1 - slot
            if step == 0 and turn_at == 0:
                pl.semaphore_wait(barrier, n)
            if turn_at + 1 == PARTS:
                send_score(step)
            send_part(step, p)
            if step == 1 and turn_at == 1:
                arrive(0)
                edge.start()
            if step == 1 and turn_at + 1 == PARTS:
                edge.wait_recv()
                add_up(0)
    if tiles == 1:
        arrive(0)
        edge.start()
        edge.wait_recv()
        add_up(0)
    for step in range(1, tiles):
        arrive(step)
        add_up(step)
        fix_up(step - 1)
    if tiles > 1:
        fixes.start()
    for step in range(tiles):
        for d in range(half):
            other_score_from(step, d).wait_recv()
        partial(step).wait_recv()
        near, far = shares(step)
        at = pl.ds(pl.multiple_of(tile_at(step, tiles) * lines, lines), lines)
        for k in range(3):
            joined_out[k, :, at] = near * part_near[step, k] + far * part_got[step, k]
    if tiles > 1:
        fixes.wait_recv()
        for step in range(tiles - 1):
            near, far = shares(step)
            fixed = near * fix_near[...] + far * fix_got[...]
            at = pl.ds(pl.multiple_of(tile_at(step, tiles) * lines, lines), lines)
            for k in range(2):
                for i in range(rows // 8):
                    moved = pltpu.roll(fixed, (lines - 2 * fix_at(step, k, i)) % lines, 1)
                    moved = jnp.where(t == 0, moved, pltpu.roll(moved, lines - 2, 1))
                    to = pl.ds(i * 8, 8)
                    joined_out[k, to, at] = jnp.where(facing, moved, joined_out[k, to, at])
    for step in range(tiles):
        partial(step).wait_send()
        scores_sent(step).wait_send()
        all_sent(step).wait_send()
    if tiles > 1:
        fixes.wait_send()
    edge.wait_send()


def fused(n, spectra, block_scales, retina, qblock, bias):
    _, repeats, lines, samples = spectra.shape
    tiles = lines // ABLK
    inner = samples // CLASSES
    cols = repeats * ABLK
    rows = DEPTH // n
    half = n // 2
    smem = pl.BlockSpec(memory_space=pltpu.SMEM)
    return pl.pallas_call(
        fused_kernel,
        out_shape=jax.ShapeDtypeStruct((3, rows, lines), jnp.float32),
        in_specs=[
            smem, smem, smem,
            pl.BlockSpec(memory_space=pl.ANY),
            pl.BlockSpec(memory_space=pltpu.VMEM),
        ],
        out_specs=pl.BlockSpec(memory_space=pltpu.VMEM),
        scratch_shapes=[
            pltpu.VMEM((tiles, repeats, ABLK, samples), jnp.bfloat16),
            pltpu.VMEM((tiles, samples // 256, 8, cols), jnp.float32),
            pltpu.VMEM((PARTS, CLASSES, LHS, inner), jnp.bfloat16),
            pltpu.VMEM((CLASSES, 8, inner), jnp.float32),
            pltpu.VMEM((2, DBLK + 8, inner), jnp.float32),
            pltpu.VMEM((2, DBLK + 8, 128), jnp.float32),
            pltpu.VMEM((256, 256), jnp.bfloat16),
            pltpu.VMEM((CLASSES, inner, cols), jnp.bfloat16),
            pltpu.VMEM((CLASSES, inner, cols), jnp.bfloat16),
            pltpu.VMEM((CLASSES, LHS, cols), jnp.float32),
            pltpu.VMEM((CLASSES, LHS, cols), jnp.float32),
            pltpu.VMEM((2, 2, 8, ABLK), jnp.float32),
            pltpu.VMEM((8, ABLK), jnp.float32),
            pltpu.VMEM((tiles, PARTS, NDB, 2, PART, ABLK), jnp.float32),
            pltpu.VMEM((tiles, half, 2, 2, rows, ABLK), jnp.float32),
            pltpu.VMEM((tiles, 8, ABLK), jnp.float32),
            pltpu.VMEM((tiles, n, 8, ABLK), jnp.float32),
            pltpu.VMEM((tiles, 3, rows, ABLK), jnp.float32),
            pltpu.VMEM((tiles, 3, rows, ABLK), jnp.float32),
            pltpu.VMEM((tiles, 3, rows, ABLK), jnp.float32),
            pltpu.VMEM((half, 2, rows, ABLK), jnp.float32),
            pltpu.VMEM((8, ABLK), jnp.float32),
            pltpu.VMEM((8, ABLK), jnp.float32),
            pltpu.VMEM((8, ABLK), jnp.float32),
            pltpu.SemaphoreType.DMA((tiles,)),
            pltpu.SemaphoreType.DMA((tiles,)),
            pltpu.SemaphoreType.DMA((tiles, half)),
            pltpu.SemaphoreType.DMA((tiles,)),
            pltpu.SemaphoreType.DMA((tiles, n)),
            pltpu.SemaphoreType.DMA((tiles,)),
            pltpu.SemaphoreType.DMA((tiles,)),
            pltpu.SemaphoreType.DMA((2, tiles)),
            pltpu.SemaphoreType.DMA((2,)),
            pltpu.SemaphoreType.DMA((2,)),
        ],
        compiler_params=pltpu.CompilerParams(
            vmem_limit_bytes=67043328, collective_id=0, has_side_effects=True
        ),
    )(retina.T, qblock, bias, spectra, block_scales.transpose(0, 1, 3, 2))


def finish_kernel(joined, ang_out, str_out, spread_out):
    ang = joined[0]
    ang_out[...] = ang
    str_out[...] = joined[2]
    spread_out[...] = jnp.sqrt(joined[1] - ang * ang + 0.01)


def finish(joined):
    out = jax.ShapeDtypeStruct(joined.shape[1:], jnp.float32)
    return pl.pallas_call(finish_kernel, out_shape=(out, out, out))(joined)


def solution(mesh):
    n = mesh.shape["vol"]
    assert mesh.shape["tile"] == 2

    def on_device(spectra, block_scales, retina_blocks, quality_block, quality_bias):
        return finish(
            fused(n, spectra, block_scales, retina_blocks, quality_block, quality_bias)
        )

    return jax.shard_map(
        on_device,
        mesh=mesh,
        in_specs=(
            P(("study", "vol"), None, "tile", None),
            P(("study", "vol"), None, "tile", None),
            P(("study", "tile"), None),
            P(("study", "vol"), "tile"),
            P(("study", "vol"), "tile"),
        ),
        out_specs=(
            P(("study", "vol"), "tile"),
            P(("study", "vol"), "tile"),
            P(("study", "vol"), "tile"),
        ),
        check_vma=False,
    )
```

```python
import functools
import math

import jax
import jax.numpy as jnp
from jax import lax
from jax.experimental import pallas as pl
from jax.experimental.pallas import tpu as pltpu
from jax.sharding import PartitionSpec as P

DEPTH = 512
BANDS = 4
DBLK = 128
ABLK = 128
SB = 128
NDB = 4
CLASSES = 8
MESH = pl.DeviceIdType.MESH
PART = 32
PARTS = DBLK // PART
GROUPS = PART // 8
SPREAD = 2
HEAD = BANDS * 2 * PART
LHS = HEAD + 16
SPAN = PART // 2


def turn(re, im, cre, cim):
    return re * cre - im * cim, re * cim + im * cre


def build_trig(wins, trig, steps, perm, samples):
    inner = samples // CLASSES
    unit = 2.0 * math.pi / samples
    kk = (
        lax.broadcasted_iota(jnp.int32, (CLASSES, inner), 1) * CLASSES
        + lax.broadcasted_iota(jnp.int32, (CLASSES, inner), 0)
    ).astype(jnp.float32)
    for k0 in range(CLASSES):
        wins[k0] = jnp.zeros((8, inner), jnp.float32)
    for b in range(BANDS):
        distance = kk - (b + 0.5) * (samples / BANDS)
        offset = distance / (samples / 8.0)
        g = jnp.where(jnp.abs(distance) <= samples / 2.0, jnp.exp(-0.5 * offset * offset), 0.0)
        g = g / jnp.sqrt(jnp.sum(g * g, keepdims=True))
        for k0 in range(CLASSES):
            wins[k0, b : b + 1, :] = g[k0 : k0 + 1]
            wins[k0, BANDS + b : BANDS + b + 1, :] = g[k0 : k0 + 1]
    z = lax.broadcasted_iota(jnp.int32, (8, inner), 0)
    k1 = lax.broadcasted_iota(jnp.int32, (8, inner), 1)
    angle = ((CLASSES * k1 * z) % samples).astype(jnp.float32) * unit
    trig[0, :8], trig[1, :8] = jnp.cos(angle), -jnp.sin(angle)
    angle = ((CLASSES * k1 * 8) % samples).astype(jnp.float32) * unit
    cre, cim = jnp.cos(angle), -jnp.sin(angle)
    angle = z.astype(jnp.float32)[:, :128] * unit
    steps[0, :8], steps[1, :8] = jnp.cos(angle), -jnp.sin(angle)
    have = 8
    while have < DBLK:
        for at in range(0, have, 8):
            to = pl.ds(have + at, 8)
            trig[0, to], trig[1, to] = turn(trig[0, at : at + 8], trig[1, at : at + 8], cre, cim)
            steps[0, to], steps[1, to] = turn(
                steps[0, at : at + 8],
                steps[1, at : at + 8],
                math.cos(have * unit),
                -math.sin(have * unit),
            )
        cre, cim = turn(cre, cim, cre, cim)
        have *= 2
    last = pl.ds(DBLK, 8)
    trig[0, last], trig[1, last] = cre, cim
    steps[0, last] = jnp.full((8, 128), math.cos(DBLK * unit), jnp.float32)
    steps[1, last] = jnp.full((8, 128), -math.sin(DBLK * unit), jnp.float32)
    size = perm.shape[0]
    part = size // CLASSES
    row = lax.broadcasted_iota(jnp.int32, (size, size), 0)
    col = lax.broadcasted_iota(jnp.int32, (size, size), 1)
    perm[...] = jnp.where(col == (row % part) * CLASSES + row // part, 1.0, 0.0).astype(jnp.bfloat16)


def low_of(p, h):
    return h * (DBLK // 2) + (PARTS - 1 - p) * SPAN


def build_class(table, wins, trig, steps, k0):
    inner = trig.shape[2]
    rows = [wins[k0, b : b + 1, :] for b in range(BANDS)]
    for p in range(PARTS):
        for c in range(2):
            value = jnp.concatenate(
                [trig[c, pl.ds(low_of(p, h), SPAN)] for h in range(2)], axis=0
            )
            for b in range(BANDS):
                to = pl.ds((b * 2 + c) * PART, PART)
                table[p, k0, to, :] = (value * rows[b]).astype(jnp.bfloat16)
    last = pl.ds(DBLK, 8)
    high = lax.broadcasted_iota(jnp.int32, (8, inner), 0) < BANDS
    middle = pl.ds(DBLK // 2, 1)
    both = jnp.concatenate(
        [jnp.where(high, trig[c, last], trig[c, middle]) * wins[k0] for c in range(2)], axis=0
    )
    for p in range(PARTS):
        table[p, k0, HEAD:LHS, :] = both.astype(jnp.bfloat16)
    for at in range(0, DBLK + 8, 8):
        here = pl.ds(at, 8)
        sre = jnp.concatenate([steps[0, here]] * (inner // 128), axis=1)
        sim = jnp.concatenate([steps[1, here]] * (inner // 128), axis=1)
        trig[0, here], trig[1, here] = turn(trig[0, here], trig[1, here], sre, sim)


def combine(get):
    rr, ii = [get(k, 0) for k in range(8)], [get(k, 1) for k in range(8)]
    sr = [rr[j] + rr[j + 4] for j in range(4)]
    si = [ii[j] + ii[j + 4] for j in range(4)]
    dr = [rr[j] - rr[j + 4] for j in range(4)]
    di = [ii[j] - ii[j + 4] for j in range(4)]
    half = math.sqrt(0.5)
    re0, im0 = (sr[0] + sr[2]) + (sr[1] + sr[3]), (si[0] + si[2]) + (si[1] + si[3])
    re3, im3 = (sr[0] - sr[2]) - (si[1] - si[3]), (si[0] - si[2]) + (sr[1] - sr[3])
    p, q = (dr[1] - dr[3]) * half, (di[1] + di[3]) * half
    r, t = (di[1] - di[3]) * half, (dr[1] + dr[3]) * half
    re2, im2 = (dr[0] + di[2]) + (p + q), (di[0] - dr[2]) + (r - t)
    re1, im1 = (dr[0] - di[2]) + (p - q), (di[0] + dr[2]) + (r + t)
    fields = ((re0, im0), (re1, im1), (re2, im2), (re3, im3))
    return [re * re + (im * im + 0.05) for re, im in fields]


def ratio_and_total(powers, d):
    total = powers[0][d]
    ratio = None
    for first, second in zip(powers[:-1], powers[1:]):
        first, second = first[d], second[d]
        total = total + second
        prod, both = first * second, first + second
        term = prod * lax.rsqrt(prod * (both * both))
        ratio = term if ratio is None else ratio + term
    return ratio, total


def tile_at(step, tiles):
    t = lax.axis_index("tile")
    return (tiles - 1 - step) + t * (2 * step - tiles + 1)


def fused_kernel(
    retina, qblock, bias, spec, scales, joined_out,
    xin, factors, table, wins, trig, steps, perm, da, db, ga, gb, prev, score_acc,
    sent, got, score_sent, score_got, part_sent, part_got, part_near, redge,
    fix_sent, fix_got, fix_near,
    isem, ssem, rsem, csem, dsem, psem, qsem, lsem, esem, fsem,
):
    tiles, repeats, lines, samples = xin.shape
    chunk = perm.shape[0]
    chunks = samples // chunk
    n = score_got.shape[1]
    half = n // 2
    rows = redge.shape[2]
    me, t = lax.axis_index("vol"), lax.axis_index("tile")
    other = 1 - t
    side, place = me // half, me % half
    part = chunk // CLASSES
    cols = repeats * lines

    data, g = (da, db), (ga, gb)

    def load(step):
        at = pl.ds(pl.multiple_of(tile_at(step, tiles) * lines, lines), lines)
        return pltpu.make_async_copy(spec.at[0, :, at, :], xin.at[step], isem.at[step])

    load(0).start()
    barrier = pltpu.get_barrier_semaphore()
    for d in range(1, n):
        pl.semaphore_signal(barrier, inc=1, device_id={"vol": (me + d) % n}, device_id_type=MESH)
    pl.semaphore_signal(barrier, inc=1, device_id={"tile": other}, device_id_type=MESH)
    build_trig(wins, trig, steps, perm, samples)
    per = chunk // SB
    for step in range(tiles):
        lane = pl.ds(pl.multiple_of(tile_at(step, tiles) * lines, lines), lines)
        for r in range(repeats):
            block = scales[0, r, :, lane]
            for q in range(chunks):
                factors[step, q, :per, r * lines : (r + 1) * lines] = block[q * per : (q + 1) * per]

    def prepare(step, q):
        at = pl.ds(q * chunk if isinstance(q, int) else pl.multiple_of(q * chunk, chunk), chunk)
        block = xin[step, :, :, at].reshape(cols, chunk)
        moved = lax.dot_general(
            perm[...], block, (((1,), (1,)), ((), ())), preferred_element_type=jnp.float32
        )
        factor = jnp.concatenate(
            [
                jnp.broadcast_to(factors[step, q, h : h + 1, :], (part // per, cols))
                for h in range(per)
            ],
            axis=0,
        )
        to = pl.ds(q * part if isinstance(q, int) else pl.multiple_of(q * part, part), part)
        for k0 in range(CLASSES):
            data[step % 2][k0, to, :] = (moved[k0 * part : (k0 + 1) * part] * factor).astype(
                jnp.bfloat16
            )

    def multiply(step, p, slot, k0):
        g[slot][k0] = jnp.dot(
            table[p, k0], data[step % 2][k0], preferred_element_type=jnp.float32
        )

    sub = lax.broadcasted_iota(jnp.int32, (8, lines), 0)
    backwards = (8 - sub) % 8

    def dec_of(ratio):
        return 1.0 - ratio * (2.0 / (BANDS * (repeats - 1)))

    def struct_of(total):
        return jnp.log(total * (1.0 / (BANDS * repeats)) + 0.05)

    def lanes(r):
        return slice(r * lines, (r + 1) * lines)

    def reduce_last(slot):
        powers = [
            combine(lambda k, c: g[slot][k, HEAD + c * 8 : HEAD + c * 8 + 8, lanes(r)])
            for r in range(repeats)
        ]
        for d in (1, 3):
            ratio, total = ratio_and_total(powers, d)
            for h, those in enumerate((slice(BANDS, 2 * BANDS), slice(0, BANDS))):
                dec = dec_of(jnp.sum(ratio[those], axis=0, keepdims=True))
                struct = struct_of(jnp.sum(total[those], axis=0, keepdims=True))
                prev[h, d // 2, 0] = jnp.broadcast_to(dec, (8, lines))
                prev[h, d // 2, 1] = jnp.broadcast_to(struct, (8, lines))

    def reduce(step, p, slot, i):
        here = tile_at(step, tiles)
        first, last, rated = retina[0, here], retina[1, here], qblock[0, here]
        h = i % 2
        within = SPAN - 8 - i // 2 * 8
        at = h * SPAN + within
        ratios, totals = [None] * NDB, [None] * NDB
        for b in range(BANDS):
            powers = [
                combine(lambda k, c: g[slot][k, pl.ds((b * 2 + c) * PART + at, 8), lanes(r)])
                for r in range(repeats)
            ]
            for d in range(NDB):
                ratio, total = ratio_and_total(powers, d)
                ratios[d] = ratio if b == 0 else ratios[d] + ratio
                totals[d] = total if b == 0 else totals[d] + total
        score = score_acc[...]
        for d in range(NDB):
            dec, struct = dec_of(ratios[d]), struct_of(totals[d])
            to = within
            if d % 2:
                low_dec, low_struct = prev[h, d // 2, 0], prev[h, d // 2, 1]
                prev[h, d // 2, 0] = dec
                prev[h, d // 2, 1] = struct
                dec = jnp.where(sub == 0, low_dec, jnp.take_along_axis(dec, backwards, axis=0))
                struct = jnp.where(
                    sub == 0, low_struct, jnp.take_along_axis(struct, backwards, axis=0)
                )
                to = SPAN - 8 - within
            inside = (first <= d) & (d <= last)
            score = score + jnp.where(rated == d, struct, 0.0)
            sent[step, p, d % 2, h, d // 2, 0, pl.ds(to, 8), :] = jnp.where(inside, dec, 0.0)
            sent[step, p, d % 2, h, d // 2, 1, pl.ds(to, 8), :] = jnp.where(inside, struct, 0.0)
        score_acc[...] = score

    def goes_to(p, d, h):
        low = low_of(p, h)
        depth = d * DBLK + (DBLK - SPAN - low if d % 2 else low)
        u = depth // rows
        return u % half, depth % rows

    def maps(step, p, d, h):
        target, at = goes_to(p, d, h)
        return pltpu.make_async_remote_copy(
            src_ref=sent.at[step, p, d, h],
            dst_ref=got.at[step, place, :, :, pl.ds(at, SPAN), :],
            send_sem=ssem.at[step], recv_sem=rsem.at[step, place],
            device_id={"vol": side * half + target}, device_id_type=MESH,
        )

    def own_maps(step, p, d, h):
        target, at = goes_to(p, d, h)
        return pltpu.make_async_copy(
            sent.at[step, p, d, h], got.at[step, place, :, :, pl.ds(at, SPAN), :],
            lsem.at[0, step],
        )

    def arrived(step, source):
        return pltpu.make_async_remote_copy(
            src_ref=got.at[step, source], dst_ref=got.at[step, source],
            send_sem=ssem.at[step], recv_sem=rsem.at[step, source],
            device_id={"vol": side * half + source}, device_id_type=MESH,
        )

    def all_sent(step):
        those = got.at[step, pl.ds(0, half - 1)]
        return pltpu.make_async_remote_copy(
            src_ref=those, dst_ref=those,
            send_sem=ssem.at[step], recv_sem=rsem.at[step, 0],
            device_id={"vol": (me + 1) % n}, device_id_type=MESH,
        )

    def own_arrived(step):
        return pltpu.make_async_copy(got.at[step, place], got.at[step, place], lsem.at[0, step])

    def score_to(step, d):
        return pltpu.make_async_remote_copy(
            src_ref=score_sent.at[step], dst_ref=score_got.at[step, me],
            send_sem=csem.at[step], recv_sem=dsem.at[step, me],
            device_id={"vol": (me + d) % n}, device_id_type=MESH,
        )

    def group_score_from(step, d):
        source = side * half + (place + d) % half
        return pltpu.make_async_remote_copy(
            src_ref=score_sent.at[step], dst_ref=score_got.at[step, source],
            send_sem=csem.at[step], recv_sem=dsem.at[step, source],
            device_id={"vol": source}, device_id_type=MESH,
        )

    def other_score_from(step, d):
        source = (1 - side) * half + (place + d) % half
        return pltpu.make_async_remote_copy(
            src_ref=score_sent.at[step], dst_ref=score_got.at[step, source],
            send_sem=csem.at[step], recv_sem=dsem.at[step, source],
            device_id={"vol": source}, device_id_type=MESH,
        )

    def scores_sent(step):
        those = score_got.at[step, pl.ds(0, n - 1)]
        return pltpu.make_async_remote_copy(
            src_ref=those, dst_ref=those,
            send_sem=csem.at[step], recv_sem=dsem.at[step, 0],
            device_id={"vol": (me + 1) % n}, device_id_type=MESH,
        )

    def partial(step):
        return pltpu.make_async_remote_copy(
            src_ref=part_sent.at[step], dst_ref=part_got.at[step],
            send_sem=psem.at[step], recv_sem=qsem.at[step],
            device_id={"vol": (1 - side) * half + place}, device_id_type=MESH,
        )

    fixes = pltpu.make_async_remote_copy(
        src_ref=fix_sent, dst_ref=fix_got, send_sem=fsem.at[0], recv_sem=fsem.at[1],
        device_id={"vol": (1 - side) * half + place}, device_id_type=MESH,
    )

    edge = pltpu.make_async_remote_copy(
        src_ref=got.at[0, :, :, 0], dst_ref=redge,
        send_sem=esem.at[0], recv_sem=esem.at[1],
        device_id={"tile": other}, device_id_type=MESH,
    )

    def send_part(step, p):
        for d in range(2):
            for h in range(2):
                target, _ = goes_to(p, d, h)

                @pl.when(place != target)
                def _():
                    maps(step, p, d, h).start()

                @pl.when(place == target)
                def _():
                    own_maps(step, p, d, h).start()

    lane = lax.broadcasted_iota(jnp.int32, (8, lines), 1)
    facing = jnp.where(t == 0, lane, lines - 1 - lane) < 2

    def send_score(step):
        total = jnp.sum(score_acc[...], axis=0, keepdims=True)
        mean = jnp.sum(total, axis=1, keepdims=True) * (1.0 / (DBLK * lines))
        mean = mean + bias[0, tile_at(step, tiles)]
        score_sent[step] = jnp.broadcast_to(mean, (8, lines))
        for d in range(1, n):
            score_to(step, d).start()
        pltpu.make_async_copy(
            score_sent.at[step], score_got.at[step, me], lsem.at[1, step]
        ).start()

    def arrive(step):
        own_arrived(step).wait()
        pltpu.make_async_copy(
            score_sent.at[step], score_got.at[step, me], lsem.at[1, step]
        ).wait()
        for d in range(1, half):
            group_score_from(step, d).wait_recv()
        for d in range(1, half):
            arrived(step, (place + d) % half).wait_recv()

    def group_weights(step, at):
        ratings = [score_got[step, at * half + v, :1, :] for v in range(half)]
        top = functools.reduce(jnp.maximum, ratings)
        return top, [jnp.exp(x - top) for x in ratings]

    def shares(step):
        near_top, near_weights = group_weights(step, side)
        far_top, far_weights = group_weights(step, 1 - side)
        top = jnp.maximum(near_top, far_top)
        near, far = jnp.exp(near_top - top), jnp.exp(far_top - top)
        total = near * functools.reduce(jnp.add, near_weights)
        total = total + far * functools.reduce(jnp.add, far_weights)
        return near / total, far / total

    def smooth_of(step, v, to, at, with_next):
        own = got[step, v, to, 0, pl.ds(at, 8), :]
        if step:
            inner = got[step - 1, v, to, 0, pl.ds(at, 8), :]
        else:
            inner = redge[v, to, pl.ds(at, 8), :]
        outer = got[step + 1, v, to, 0, pl.ds(at, 8), :] if with_next else 0.0
        near_right = jnp.where(lane < lines // 2, jnp.where(t == 0, inner, outer), own)
        near_left = jnp.where(lane < lines // 2, own, jnp.where(t == 0, outer, inner))
        right2 = pltpu.roll(jnp.where(lane >= lines - 2, near_left, own), 2, 1)
        right1 = pltpu.roll(jnp.where(lane >= lines - 1, near_left, own), 1, 1)
        left1 = pltpu.roll(jnp.where(lane < 1, near_right, own), lines - 1, 1)
        left2 = pltpu.roll(jnp.where(lane < 2, near_right, own), lines - 2, 1)
        return (
            (right2 + left2) * (1.0 / 9.0) + (right1 + left1) * (2.0 / 9.0) + own * (3.0 / 9.0)
        )

    def add_up(step):
        _, weights = group_weights(step, side)
        for far in range(2):
            to = 1 - side if far else side
            store = part_sent if far else part_near
            for at in range(0, rows, 8):
                ang = square = joined = 0.0
                for v in range(half):
                    smooth = smooth_of(step, v, to, at, False)
                    ws = weights[v] * smooth
                    ang = ang + ws
                    square = square + ws * smooth
                    joined = joined + weights[v] * got[step, v, to, 1, pl.ds(at, 8), :]
                store[step, 0, at : at + 8, :] = ang
                store[step, 1, at : at + 8, :] = square
                store[step, 2, at : at + 8, :] = joined
        partial(step).start()

    def fix_at(step, k, i):
        return (step * 2 + k) * (rows // 8) + i

    assert 2 * fix_at(max(tiles - 2, 0), 1, rows // 8 - 1) + 2 <= lines

    def fix_up(step):
        _, weights = group_weights(step, side)
        for far in range(2):
            to = 1 - side if far else side
            store = fix_sent if far else fix_near
            packed = store[...] if step else jnp.zeros((8, lines), jnp.float32)
            for i in range(rows // 8):
                ang = square = 0.0
                for v in range(half):
                    smooth = smooth_of(step, v, to, i * 8, True)
                    ws = weights[v] * smooth
                    ang = ang + ws
                    square = square + ws * smooth
                for k, value in enumerate((ang, square)):
                    value = jnp.where(t == 0, value, pltpu.roll(value, 2, 1))
                    place_at = fix_at(step, k, i)
                    moved = pltpu.roll(value, 2 * place_at, 1) if place_at else value
                    packed = jnp.where(lane // 2 == place_at, moved, packed)
            store[...] = packed

    load(0).wait()
    for step in range(1, tiles):
        load(step).start()

    def first_pass(k0):
        build_class(table, wins, trig, steps, k0)
        prepare(0, k0)

    assert chunks == CLASSES and GROUPS == SPREAD * (chunks // PARTS)
    for k0 in range(CLASSES):
        first_pass(k0)
    for k0 in range(CLASSES):
        multiply(0, 0, 0, k0)
    if tiles > 1:
        load(1).wait()
        for q in range(chunks // PARTS):
            prepare(1, q)

    slot = 0
    each = CLASSES // GROUPS
    for step in range(tiles):
        score_acc[...] = jnp.zeros_like(score_acc)
        reduce_last(slot)
        for turn_at in range(PARTS):
            p = turn_at
            if turn_at + 1 < PARTS:
                following = (step, p + 1)
            elif step + 1 < tiles:
                following = (step + 1, 0)
            else:
                following = None

            if turn_at + 1 < PARTS:
                ready, first_chunk = step + 1, (turn_at + 1) * (chunks // PARTS)
            else:
                ready, first_chunk = step + 2, 0
            if ready >= tiles:
                ready = None
            elif turn_at + 1 == PARTS:
                load(ready).wait()

            def body():
                for i in range(GROUPS):
                    if following is not None:
                        for k in range(each):
                            multiply(*following, 1 - slot, i * each + k)
                    if ready is not None and (i + 1) % SPREAD == 0:
                        prepare(ready, first_chunk + i // SPREAD)
                    reduce(step, p, slot, i)

            body()
            slot = 1 - slot
            if step == 0 and turn_at == 0:
                pl.semaphore_wait(barrier, n)
            if turn_at + 1 == PARTS:
                send_score(step)
            send_part(step, p)
            if step == 1 and turn_at == 2:
                arrive(0)
                edge.start()
            if step == 1 and turn_at + 1 == PARTS:
                edge.wait_recv()
                add_up(0)
    if tiles == 1:
        arrive(0)
        edge.start()
        edge.wait_recv()
        add_up(0)
    for step in range(1, tiles):
        arrive(step)
        add_up(step)
        fix_up(step - 1)
    if tiles > 1:
        fixes.start()
    for step in range(tiles):
        for d in range(half):
            other_score_from(step, d).wait_recv()
        partial(step).wait_recv()
        near, far = shares(step)
        at = pl.ds(pl.multiple_of(tile_at(step, tiles) * lines, lines), lines)
        for k in range(3):
            joined_out[k, :, at] = near * part_near[step, k] + far * part_got[step, k]
    if tiles > 1:
        fixes.wait_recv()
        for step in range(tiles - 1):
            near, far = shares(step)
            fixed = near * fix_near[...] + far * fix_got[...]
            at = pl.ds(pl.multiple_of(tile_at(step, tiles) * lines, lines), lines)
            for k in range(2):
                for i in range(rows // 8):
                    moved = pltpu.roll(fixed, (lines - 2 * fix_at(step, k, i)) % lines, 1)
                    moved = jnp.where(t == 0, moved, pltpu.roll(moved, lines - 2, 1))
                    to = pl.ds(i * 8, 8)
                    joined_out[k, to, at] = jnp.where(facing, moved, joined_out[k, to, at])
    for step in range(tiles):
        partial(step).wait_send()
        scores_sent(step).wait_send()
        all_sent(step).wait_send()
    if tiles > 1:
        fixes.wait_send()
    edge.wait_send()


def fused(n, spectra, block_scales, retina, qblock, bias):
    _, repeats, lines, samples = spectra.shape
    tiles = lines // ABLK
    inner = samples // CLASSES
    cols = repeats * ABLK
    rows = DEPTH // n
    half = n // 2
    smem = pl.BlockSpec(memory_space=pltpu.SMEM)
    return pl.pallas_call(
        fused_kernel,
        out_shape=jax.ShapeDtypeStruct((3, rows, lines), jnp.float32),
        in_specs=[
            smem, smem, smem,
            pl.BlockSpec(memory_space=pl.ANY),
            pl.BlockSpec(memory_space=pltpu.VMEM),
        ],
        out_specs=pl.BlockSpec(memory_space=pltpu.VMEM),
        scratch_shapes=[
            pltpu.VMEM((tiles, repeats, ABLK, samples), jnp.bfloat16),
            pltpu.VMEM((tiles, samples // 256, 8, cols), jnp.float32),
            pltpu.VMEM((PARTS, CLASSES, LHS, inner), jnp.bfloat16),
            pltpu.VMEM((CLASSES, 8, inner), jnp.float32),
            pltpu.VMEM((2, DBLK + 8, inner), jnp.float32),
            pltpu.VMEM((2, DBLK + 8, 128), jnp.float32),
            pltpu.VMEM((256, 256), jnp.bfloat16),
            pltpu.VMEM((CLASSES, inner, cols), jnp.bfloat16),
            pltpu.VMEM((CLASSES, inner, cols), jnp.bfloat16),
            pltpu.VMEM((CLASSES, LHS, cols), jnp.float32),
            pltpu.VMEM((CLASSES, LHS, cols), jnp.float32),
            pltpu.VMEM((2, 2, 2, 8, ABLK), jnp.float32),
            pltpu.VMEM((8, ABLK), jnp.float32),
            pltpu.VMEM((tiles, PARTS, 2, 2, 2, 2, SPAN, ABLK), jnp.float32),
            pltpu.VMEM((tiles, half, 2, 2, rows, ABLK), jnp.float32),
            pltpu.VMEM((tiles, 8, ABLK), jnp.float32),
            pltpu.VMEM((tiles, n, 8, ABLK), jnp.float32),
            pltpu.VMEM((tiles, 3, rows, ABLK), jnp.float32),
            pltpu.VMEM((tiles, 3, rows, ABLK), jnp.float32),
            pltpu.VMEM((tiles, 3, rows, ABLK), jnp.float32),
            pltpu.VMEM((half, 2, rows, ABLK), jnp.float32),
            pltpu.VMEM((8, ABLK), jnp.float32),
            pltpu.VMEM((8, ABLK), jnp.float32),
            pltpu.VMEM((8, ABLK), jnp.float32),
            pltpu.SemaphoreType.DMA((tiles,)),
            pltpu.SemaphoreType.DMA((tiles,)),
            pltpu.SemaphoreType.DMA((tiles, half)),
            pltpu.SemaphoreType.DMA((tiles,)),
            pltpu.SemaphoreType.DMA((tiles, n)),
            pltpu.SemaphoreType.DMA((tiles,)),
            pltpu.SemaphoreType.DMA((tiles,)),
            pltpu.SemaphoreType.DMA((2, tiles)),
            pltpu.SemaphoreType.DMA((2,)),
            pltpu.SemaphoreType.DMA((2,)),
        ],
        compiler_params=pltpu.CompilerParams(
            vmem_limit_bytes=67043328, collective_id=0, has_side_effects=True
        ),
    )(retina.T, qblock, bias, spectra, block_scales.transpose(0, 1, 3, 2))


def finish_kernel(joined, ang_out, str_out, spread_out):
    ang = joined[0]
    ang_out[...] = ang
    str_out[...] = joined[2]
    spread_out[...] = jnp.sqrt(joined[1] - ang * ang + 0.01)


def finish(joined):
    out = jax.ShapeDtypeStruct(joined.shape[1:], jnp.float32)
    return pl.pallas_call(finish_kernel, out_shape=(out, out, out))(joined)


def solution(mesh):
    n = mesh.shape["vol"]
    assert mesh.shape["tile"] == 2

    def on_device(spectra, block_scales, retina_blocks, quality_block, quality_bias):
        return finish(
            fused(n, spectra, block_scales, retina_blocks, quality_block, quality_bias)
        )

    return jax.shard_map(
        on_device,
        mesh=mesh,
        in_specs=(
            P(("study", "vol"), None, "tile", None),
            P(("study", "vol"), None, "tile", None),
            P(("study", "tile"), None),
            P(("study", "vol"), "tile"),
            P(("study", "vol"), "tile"),
        ),
        out_specs=(
            P(("study", "vol"), "tile"),
            P(("study", "vol"), "tile"),
            P(("study", "vol"), "tile"),
        ),
        check_vma=False,
    )
```
